512 devices in a mesh: shards: 16 (over z, core), tensor: 4 (over x), sections: 8 (over y).
Axes of the slice: x: 4, y: 8, z: 8, core: 2. Of those that a mesh axis runs over, the one named last changes fastest.
Arguments:
- replica_grads: bfloat16 [16, 8, 2, 1536, 512], P('shards', 'sections', None, None, 'tensor'), may hold values from -6 to 6
- error_feedback: bfloat16 [16, 8, 2, 1536, 512], P('shards', 'sections', None, None, 'tensor'), may hold values from -3 to 3
- q_start: float32 [8, 2, 512, 32], P('sections', None, 'tensor'), may hold values from -0.25 to 0.25
- gram_root: float32 [8, 2, 32, 32], P('sections'), may hold values from -2 to 2
- momentum: float32 [8, 2, 1536, 512], P('sections', None, 'shards', 'tensor'), may hold values from -1.2 to 1.2
- weights: float32 [8, 2, 1536, 512], P('sections', None, 'shards', 'tensor'), may hold values from -3 to 3
- router_partials: bfloat16 [512, 1536, 40], P(('shards', 'tensor', 'sections')), may hold values from -12 to 12
- gain_partials: bfloat16 [512, 2, 1536], P(('shards', 'tensor', 'sections')), may hold values from -12 to 12
- router_momentum: float32 [1536, 40], P('shards'), may hold values from -1.2 to 1.2
- router_weights: float32 [1536, 40], P('shards'), may hold values from -3 to 3
- gain_momentum: float32 [2, 1536], P(None, 'shards'), may hold values from -1.2 to 1.2
- gain_weights: float32 [2, 1536], P(None, 'shards'), may hold values from 0.1 to 1.9
Outputs:
- new_error: bfloat16 [16, 8, 2, 1536, 512], P('shards', 'sections', None, None, 'tensor')
- new_momentum: float32 [8, 2, 1536, 512], P('sections', None, 'shards', 'tensor')
- new_weights: float32 [8, 2, 1536, 512], P('sections', None, None, 'tensor')
- new_router_momentum: float32 [1536, 40], P('shards')
- new_router_weights: float32 [1536, 40], replicated
- new_gain_momentum: float32 [2, 1536], P(None, 'shards')
- new_gain_weights: float32 [2, 1536], replicated
The draws below stay inside these ranges and needn't reach their ends.
All inputs are finite; a program needn't handle non-finite values.
Results may differ from the reference program's by a relative error of at most 0.001.
Values sent between devices are 32-bit elements; how exact they have to be, the bound alone decides.
No kernel may reach another device: no remote copies, remote signals or barrier semaphores. Data moves between devices by JAX's collectives and lax.ppermute only.
A program may use at most 64 MiB of HBM per device.

```python
import jax
import jax.numpy as jnp
from jax import lax

D = 1536
FF = 512
NE = 40
R = 32
EXPERTS = 8
GROUPS = 512
N_SHARDS = 16


def draw_gram_root(key, part):
    first_key, second_key = jax.random.split(key)
    factor = 3.0 / (D * R) ** 0.25
    offdiag = 0.35 * jax.random.normal(first_key, (EXPERTS, 2, R, R), jnp.float32) / R ** 0.5
    diagonal = 1.0 + 0.5 * jax.random.uniform(second_key, (EXPERTS, 2, R), jnp.float32)
    identity = jnp.eye(R, dtype=jnp.float32)
    return factor * (offdiag + identity * diagonal[..., None])


def spiked(array, own_key, source, target, parts, factor):
    owner, partner = [(jnp.arange(array.shape[axis_at]) // (array.shape[axis_at] // parts)).reshape([-1 if axis == axis_at else 1 for axis in range(array.ndim)]) for axis_at in (source, target)]
    chosen = jax.random.permutation(own_key, parts)[partner]
    strong = (owner == chosen) | (owner == (partner + parts // 2) % parts)
    return jnp.where(strong, factor * array, array)


def steps_of(stream_key, dims, shards, low, top_value):
    loudness, own = 1.0, jax.random.fold_in(stream_key, 6)
    for dim, parts in shards:
        heights = jnp.exp(jax.random.uniform(jax.random.fold_in(own, dim), (parts,), jnp.float32, low / len(shards), top_value / len(shards)))
        loudness = loudness * jnp.repeat(heights, dims[dim] // parts).reshape([-1 if axis == dim else 1 for axis in range(len(dims))])
    return loudness


def gaussian(stream_key, extent, deviation, most, pieces=(), kind=jnp.bfloat16):
    level = steps_of(stream_key, extent, pieces, -0.22, 0.18) if pieces else 1.0
    array = jax.random.normal(stream_key, extent, jnp.float32) * deviation * level
    return jnp.minimum(jnp.maximum(array, -most), most).astype(kind)


def heavy_noise(rng, extent, deviation, limit, cuts, heavy, kind=jnp.bfloat16):
    values = deviation * jax.random.normal(rng, extent, jnp.float32)
    if cuts:
        values = values * steps_of(rng, extent, cuts, -0.22, 0.18)
    return jnp.clip(spiked(values, jax.random.fold_in(rng, 3), *heavy), -limit, limit).astype(kind)


def setup_inputs(seed: int = 0) -> dict:
    seeds = jax.random.split(jax.random.key(seed), 13)
    return {
        "replica_grads": gaussian(seeds[0], (N_SHARDS, EXPERTS, 2, D, FF), 1.0, 6.0, ((0, 16), (1, 8), (4, 4))),
        "error_feedback": gaussian(seeds[1], (N_SHARDS, EXPERTS, 2, D, FF), 0.5, 3.0, ((0, 16), (1, 8), (4, 4))),
        "q_start": gaussian(seeds[2], (EXPERTS, 2, FF, R), FF ** -0.5, 0.25, ((0, 8), (2, 4)), jnp.float32),
        "gram_root": draw_gram_root(jax.random.fold_in(seeds[12], 71), 0),
        "momentum": gaussian(seeds[4], (EXPERTS, 2, D, FF), 0.2, 1.2, ((0, 8), (2, 16), (3, 4)), jnp.float32),
        "weights": gaussian(seeds[5], (EXPERTS, 2, D, FF), 0.5, 3.0, ((0, 8), (2, 16), (3, 4)), jnp.float32),
        "router_partials": heavy_noise(seeds[6], (GROUPS, D, NE), 0.5, 12.0, ((0, 512),), (0, 1, 512, 6.0)),
        "gain_partials": heavy_noise(seeds[7], (GROUPS, 2, D), 0.5, 12.0, ((0, 512),), (0, 2, 512, 6.0)),
        "router_momentum": gaussian(seeds[8], (D, NE), 0.2, 1.2, ((0, 16),), jnp.float32),
        "router_weights": gaussian(seeds[9], (D, NE), 0.5, 3.0, ((0, 16),), jnp.float32),
        "gain_momentum": gaussian(seeds[10], (2, D), 0.2, 1.2, ((1, 16),), jnp.float32),
        "gain_weights": jnp.clip(1.0 + 0.18 * jax.random.normal(seeds[11], (2, D), jnp.float32), 0.1, 1.9),
    }


momentum_decay = 0.9
step_size = 0.5


def one_expert(items):
    grads, errors, q_first, root, mom, wts = items
    combined = grads.astype(jnp.float32) + errors.astype(jnp.float32)
    p_avg = jnp.einsum('skdf,kfr->kdr', combined, q_first, precision=lax.Precision.HIGHEST) / N_SHARDS
    p_hat = jnp.einsum('kdr,krt->kdt', p_avg, root, precision=lax.Precision.HIGHEST)
    q_avg = jnp.einsum('skdf,kdr->kfr', combined, p_hat, precision=lax.Precision.HIGHEST) / N_SHARDS
    approx = jnp.einsum('kdr,kfr->kdf', p_hat, q_avg, precision=lax.Precision.HIGHEST)
    new_err = (combined - approx[None]).astype(jnp.bfloat16)
    new_mom = momentum_decay * mom + approx
    new_wts = wts - step_size * new_mom
    return new_err, new_mom, new_wts


def reference(replica_grads, error_feedback, q_start, gram_root, momentum, weights, router_partials, gain_partials, router_momentum, router_weights, gain_momentum, gain_weights):
    new_err, new_mom, new_wts = lax.map(one_expert, (jnp.swapaxes(replica_grads, 0, 1), jnp.swapaxes(error_feedback, 0, 1), q_start, gram_root, momentum, weights))
    new_error = jnp.swapaxes(new_err, 0, 1)
    router_avg = jnp.sum(router_partials.astype(jnp.float32), axis=0) / N_SHARDS
    gain_avg = jnp.sum(gain_partials.astype(jnp.float32), axis=0) / N_SHARDS
    router_mom = momentum_decay * router_momentum + router_avg
    gain_mom = momentum_decay * gain_momentum + gain_avg
    router_new = router_weights - step_size * router_mom
    gain_new = gain_weights - step_size * gain_mom
    return (new_error, new_mom, new_wts, router_mom, router_new, gain_mom, gain_new)
```

```python
import jax
import jax.numpy as jnp
from jax import lax
from jax.sharding import PartitionSpec as P

momentum_decay = 0.9
step_size = 0.5
lanes = 128
rank = 32
highest = lax.Precision.HIGHEST
f32 = jnp.float32
plane = ("shards", "tensor")
sheet = ("tensor", "sections")


def exchange(blocks, axes):
    return lax.all_to_all(blocks, axes, 0, 0, tiled=True)


def spread(row, count, axes):
    return exchange(jnp.broadcast_to(row, (count,) + row.shape[1:]), axes)


def per_device(
    replica_grads,
    error_feedback,
    q_start,
    gram_root,
    momentum,
    weights,
    router_partials,
    gain_partials,
    router_momentum,
    router_weights,
    gain_momentum,
    gain_weights,
):
    shard_count = lax.axis_size("shards")
    tensor_count = lax.axis_size("tensor")
    section_count = lax.axis_size("sections")
    plane_count = shard_count * tensor_count
    sheet_count = tensor_count * section_count
    shard_index = lax.axis_index("shards")
    rows = momentum.shape[2]
    width = gain_partials.shape[2]
    start = shard_index * rows
    blocks = width // lanes

    base_rows = weights[0] - (step_size * momentum_decay) * momentum[0]
    base = lax.all_gather(base_rows, "shards", axis=1, tiled=True)

    columns = jnp.concatenate([router_partials[0].T, gain_partials[0]], 0).astype(f32)
    count = columns.shape[0]
    strips = columns.reshape(count, blocks, lanes).transpose(1, 0, 2).reshape(count * blocks, lanes)
    total_rows = plane_count * section_count
    strips = jnp.pad(strips, ((0, total_rows - count * blocks), (0, 0)))
    strips = strips.reshape(tensor_count, section_count, shard_count, lanes).transpose(1, 2, 0, 3)
    strips = strips.reshape(section_count, plane_count, lanes)
    strips = exchange(strips, "sections").sum(0)

    combined = replica_grads[0, 0].astype(f32) + error_feedback[0, 0].astype(f32)
    q_rows = q_start[0].transpose(0, 2, 1)
    p_rows = jnp.einsum("krf,kdf->krd", q_rows, combined, precision=highest)
    p_row = exchange(p_rows.reshape(plane_count, width), plane).sum(0, keepdims=True)
    packed = jnp.concatenate([jnp.broadcast_to(p_row, (plane_count, width)), strips], 1)
    packed = exchange(packed, plane)
    strip = packed[:, width:].sum(0, keepdims=True)
    p_avg = packed[:, :width].reshape(2, rank, width) / shard_count
    p_hat = jnp.einsum("krd,krt->ktd", p_avg, gram_root[0], precision=highest)
    q_local = jnp.einsum("ktd,kdf->ktf", p_hat, combined, precision=highest)

    small_base = jnp.concatenate(
        [
            router_weights.T - (step_size * momentum_decay) * router_momentum.T,
            gain_weights - (step_size * momentum_decay) * gain_momentum,
        ],
        0,
    )
    small_base = jnp.pad(small_base, ((0, 48 - count), (0, lanes - rows)))
    bundle = jnp.concatenate([q_local.reshape(2 * rank, lanes), small_base, jnp.pad(strip, ((0, 7), (0, 0)))], 0)
    bundle = lax.all_gather(bundle, "shards", axis=0, tiled=False)
    q_avg = (bundle[:, : 2 * rank].sum(0) / shard_count).reshape(2, rank, lanes)
    strip_set = bundle[:, 2 * rank + 48]
    small_base = bundle[:, 2 * rank : 2 * rank + count, :rows].transpose(1, 0, 2).reshape(count, width)

    small = spread(strip_set[None], sheet_count, sheet)
    small = small.reshape(total_rows, lanes)[: count * blocks]
    small = small.reshape(blocks, count, lanes).transpose(1, 0, 2).reshape(count, width) / shard_count

    approx = jnp.einsum("ktd,ktf->kdf", p_hat, q_avg, precision=highest)
    new_error = (combined - approx).astype(jnp.bfloat16)[None, None]
    new_weights = (base - step_size * approx)[None]
    approx_rows = lax.dynamic_slice_in_dim(approx, start, rows, 1)
    new_momentum = momentum_decay * momentum + approx_rows[None]

    own = lax.dynamic_slice_in_dim(small, start, rows, 1)
    new_router_momentum = momentum_decay * router_momentum + own[:-2].T
    new_gain_momentum = momentum_decay * gain_momentum + own[-2:]
    new_small = small_base - step_size * small
    return (
        new_error,
        new_momentum,
        new_weights,
        new_router_momentum,
        new_small[:-2].T,
        new_gain_momentum,
        new_small[-2:],
    )


def solution(mesh):
    return jax.shard_map(
        per_device,
        mesh=mesh,
        in_specs=(
            P("shards", "sections", None, None, "tensor"),
            P("shards", "sections", None, None, "tensor"),
            P("sections", None, "tensor", None),
            P("sections", None, None, None),
            P("sections", None, "shards", "tensor"),
            P("sections", None, "shards", "tensor"),
            P(("shards", "tensor", "sections"), None, None),
            P(("shards", "tensor", "sections"), None, None),
            P("shards", None),
            P("shards", None),
            P(None, "shards"),
            P(None, "shards"),
        ),
        out_specs=(
            P("shards", "sections", None, None, "tensor"),
            P("sections", None, "shards", "tensor"),
            P("sections", None, None, "tensor"),
            P("shards", None),
            P(),
            P(None, "shards"),
            P(),
        ),
        check_vma=False,
    )
```

```python
import jax
import jax.numpy as jnp
from jax import lax
from jax.experimental import pallas as pl
from jax.experimental.pallas import tpu as pltpu
from jax.sharding import PartitionSpec as P

momentum_decay = 0.9
step_size = 0.5
decayed_step = step_size * momentum_decay
lanes = 128
rank = 32
padded_columns = 48
highest = lax.Precision.HIGHEST
f32 = jnp.float32
plane = ("shards", "tensor")


def exchange(blocks, axes):
    return lax.all_to_all(blocks, axes, 0, 0, tiled=True)


def spread(row, count, axes):
    return exchange(jnp.broadcast_to(row, (count,) + row.shape[1:]), axes)


def prepare_kernel(
    weights, momentum, router_weights, router_momentum, gain_weights, gain_momentum, router, gain, base, strips
):
    rows = weights.shape[0]
    columns, part = router_weights.shape
    gains = gain_weights.shape[0]
    base[:rows] = weights[...] - decayed_step * momentum[...]
    base[rows:] = jnp.zeros((padded_columns, lanes), f32)
    base[rows : rows + columns, :part] = router_weights[...] - decayed_step * router_momentum[...]
    base[rows + columns : rows + columns + gains, :part] = gain_weights[...] - decayed_step * gain_momentum[...]
    blocks = router.shape[1] // lanes
    strips[blocks * (columns + gains) :] = jnp.zeros((strips.shape[0] - blocks * (columns + gains), lanes), f32)
    for i in range(blocks):
        cut = slice(i * lanes, (i + 1) * lanes)
        strips[i * columns : (i + 1) * columns] = router[:, cut].astype(f32)
        row = blocks * columns + i * gains
        strips[row : row + gains] = gain[:, cut].astype(f32)


def finish_kernel(
    index,
    q_set,
    p_hat,
    grads,
    errors,
    base,
    small_base,
    momentum,
    small,
    router_momentum,
    gain_momentum,
    new_error,
    new_momentum,
    new_weights,
    new_router_momentum,
    new_router_weights,
    new_gain_momentum,
    new_gain_weights,
    approx,
    average,
    start,
):
    shards = q_set.shape[0]
    rows = momentum.shape[1]
    q_avg = jnp.sum(q_set[...], 0) / shards
    approx[...] = lax.dot_general(
        p_hat[0], q_avg, (((0,), (0,)), ((), ())), precision=highest, preferred_element_type=f32
    )
    new_error[0] = (grads[0].astype(f32) + errors[0].astype(f32) - approx[...]).astype(jnp.bfloat16)
    new_weights[0] = base[...].reshape(approx.shape) - step_size * approx[...]
    own = pl.ds(pl.multiple_of(index[0] * rows, 8), rows)
    new_momentum[0] = momentum_decay * momentum[0] + approx[own]

    @pl.when(pl.program_id(0) == 0)
    def _():
        columns = router_momentum.shape[0]
        gains = gain_momentum.shape[0]
        blocks = average.shape[1] // lanes
        count = columns + gains
        for i in range(blocks):
            cut = slice(i * lanes, (i + 1) * lanes)
            average[:columns, cut] = small[i * columns : (i + 1) * columns] / shards
            row = blocks * columns + i * gains
            average[columns:count, cut] = small[row : row + gains] / shards
        mine = jnp.zeros((count, rows), f32)
        for i in range(shards):
            cut = slice(i * rows, (i + 1) * rows)
            start[:count, cut] = small_base[i, :count, :rows]
            mine = jnp.where(index[0] == i, average[:count, cut], mine)
        new_router_weights[...] = start[:columns] - step_size * average[:columns]
        new_gain_weights[...] = start[columns:count] - step_size * average[columns:count]
        new_router_momentum[...] = momentum_decay * router_momentum[...] + mine[:columns]
        new_gain_momentum[...] = momentum_decay * gain_momentum[...] + mine[columns:]


def per_device(
    replica_grads,
    error_feedback,
    q_start,
    gram_root,
    momentum,
    weights,
    router_partials,
    gain_partials,
    router_momentum,
    router_weights,
    gain_momentum,
    gain_weights,
):
    shard_count = lax.axis_size("shards")
    section_count = lax.axis_size("sections")
    plane_count = shard_count * lax.axis_size("tensor")
    index = lax.axis_index("shards").astype(jnp.int32)[None]
    pairs, rows = momentum.shape[1:3]
    columns = router_weights.shape[1]
    gains = gain_weights.shape[0]
    width = gain_partials.shape[2]
    held = pairs * rows + padded_columns

    base, strips = pl.pallas_call(
        prepare_kernel,
        out_shape=(
            jax.ShapeDtypeStruct((held, lanes), f32),
            jax.ShapeDtypeStruct((plane_count * section_count, lanes), f32),
        ),
        name="prepare",
    )(
        weights.reshape(pairs * rows, lanes),
        momentum.reshape(pairs * rows, lanes),
        router_weights.T,
        router_momentum.T,
        gain_weights,
        gain_momentum,
        router_partials[0].T,
        gain_partials[0],
    )
    base = lax.all_gather(base, "shards", axis=0, tiled=False)

    strips = exchange(strips.reshape(section_count, plane_count, lanes), "sections").sum(0)
    combined = replica_grads[0, 0].astype(f32) + error_feedback[0, 0].astype(f32)
    q_rows = q_start[0].transpose(0, 2, 1)
    p_rows = jnp.einsum("krf,kdf->krd", q_rows, combined, precision=highest)
    packed = jnp.concatenate([p_rows.reshape(plane_count, width), strips], 1)
    packed = exchange(packed, plane).sum(0, keepdims=True)
    packed = spread(packed, plane_count, plane)
    small = spread(packed[:, width:][None], section_count, "sections")

    p_avg = packed[:, :width].reshape(pairs, rank, width) / shard_count
    p_hat = jnp.einsum("krd,krt->ktd", p_avg, gram_root[0], precision=highest)
    q_local = jnp.einsum("ktd,kdf->ktf", p_hat, combined, precision=highest)
    bundle = q_local.reshape(pairs * rank, lanes)
    bundle, base = lax.optimization_barrier((bundle, base))
    q_set = lax.all_gather(bundle, "shards", axis=0, tiled=False)
    q_set, small = lax.optimization_barrier((q_set, small))

    def whole(*shape):
        return pl.BlockSpec(shape, lambda k, _: (0,) * len(shape))

    def kth(*shape):
        return pl.BlockSpec((1,) + shape, lambda k, _: (k,) + (0,) * len(shape))

    new_error, new_momentum, new_weights, router_step, router_new, gain_step, gain_new = pl.pallas_call(
        finish_kernel,
        grid_spec=pltpu.PrefetchScalarGridSpec(
            num_scalar_prefetch=1,
            grid=(pairs,),
            in_specs=[
                pl.BlockSpec((shard_count, rank, lanes), lambda k, _: (0, k, 0)),
                kth(rank, width),
                kth(width, lanes),
                kth(width, lanes),
                pl.BlockSpec((shard_count, rows, lanes), lambda k, _: (0, k, 0)),
                pl.BlockSpec(
                    (shard_count, padded_columns, lanes), lambda k, _: (0, pairs * rows // padded_columns, 0)
                ),
                kth(rows, lanes),
                whole(plane_count * section_count, lanes),
                whole(columns, rows),
                whole(gains, rows),
            ],
            out_specs=[
                kth(width, lanes),
                kth(rows, lanes),
                kth(width, lanes),
                whole(columns, rows),
                whole(columns, width),
                whole(gains, rows),
                whole(gains, width),
            ],
            scratch_shapes=[
                pltpu.VMEM((width, lanes), f32),
                pltpu.VMEM((padded_columns, width), f32),
                pltpu.VMEM((padded_columns, width), f32),
            ],
        ),
        out_shape=(
            jax.ShapeDtypeStruct((pairs, width, lanes), jnp.bfloat16),
            jax.ShapeDtypeStruct((pairs, rows, lanes), f32),
            jax.ShapeDtypeStruct((pairs, width, lanes), f32),
            jax.ShapeDtypeStruct((columns, rows), f32),
            jax.ShapeDtypeStruct((columns, width), f32),
            jax.ShapeDtypeStruct((gains, rows), f32),
            jax.ShapeDtypeStruct((gains, width), f32),
        ),
        name="finish",
    )(
        index,
        q_set,
        p_hat,
        replica_grads[0, 0],
        error_feedback[0, 0],
        base,
        base,
        momentum[0],
        small.reshape(plane_count * section_count, lanes),
        router_momentum.T,
        gain_momentum,
    )
    return (
        new_error[None, None],
        new_momentum[None],
        new_weights[None],
        router_step.T,
        router_new.T,
        gain_step,
        gain_new,
    )


def solution(mesh):
    return jax.shard_map(
        per_device,
        mesh=mesh,
        in_specs=(
            P("shards", "sections", None, None, "tensor"),
            P("shards", "sections", None, None, "tensor"),
            P("sections", None, "tensor", None),
            P("sections", None, None, None),
            P("sections", None, "shards", "tensor"),
            P("sections", None, "shards", "tensor"),
            P(("shards", "tensor", "sections"), None, None),
            P(("shards", "tensor", "sections"), None, None),
            P("shards", None),
            P("shards", None),
            P(None, "shards"),
            P(None, "shards"),
        ),
        out_specs=(
            P("shards", "sections", None, None, "tensor"),
            P("sections", None, "shards", "tensor"),
            P("sections", None, None, "tensor"),
            P("shards", None),
            P(),
            P(None, "shards"),
            P(),
        ),
        check_vma=False,
    )
```

```python
import jax
import jax.numpy as jnp
from jax import lax
from jax.experimental import pallas as pl
from jax.experimental.pallas import tpu as pltpu
from jax.sharding import Mesh
from jax.sharding import PartitionSpec as P

momentum_decay = 0.9
step_size = 0.5
decayed_step = step_size * momentum_decay
lanes = 128
rank = 32
padded_columns = 48
highest = lax.Precision.HIGHEST
f32 = jnp.float32
shards = ("stack", "core")
layer = ("stack", "tensor")


def exchange(blocks, axes):
    return lax.all_to_all(blocks, axes, 0, 0, tiled=True)


def spread(row, count, axes):
    return exchange(jnp.broadcast_to(row, (count,) + row.shape[1:]), axes)


def prepare_kernel(
    weights, momentum, router_weights, router_momentum, gain_weights, gain_momentum, router, gain, base, strips
):
    rows = weights.shape[0]
    columns, part = router_weights.shape
    gains = gain_weights.shape[0]
    base[:rows] = weights[...] - decayed_step * momentum[...]
    base[rows:] = jnp.zeros((padded_columns, lanes), f32)
    base[rows : rows + columns, :part] = router_weights[...] - decayed_step * router_momentum[...]
    base[rows + columns : rows + columns + gains, :part] = gain_weights[...] - decayed_step * gain_momentum[...]
    blocks = router.shape[1] // lanes
    strips[blocks * (columns + gains) :] = jnp.zeros((strips.shape[0] - blocks * (columns + gains), lanes), f32)
    for i in range(blocks):
        cut = slice(i * lanes, (i + 1) * lanes)
        strips[i * columns : (i + 1) * columns] = router[:, cut].astype(f32)
        row = blocks * columns + i * gains
        strips[row : row + gains] = gain[:, cut].astype(f32)


def pieces(value):
    high = value.astype(jnp.bfloat16)
    rest = value - high.astype(f32)
    mid = rest.astype(jnp.bfloat16)
    return high, mid, (rest - mid.astype(f32)).astype(jnp.bfloat16)


def finish_kernel(
    index,
    q_set,
    p_hat,
    grads,
    errors,
    base,
    small_base,
    momentum,
    small,
    router_momentum,
    gain_momentum,
    new_error,
    new_momentum,
    new_weights,
    new_router_momentum,
    new_router_weights,
    new_gain_momentum,
    new_gain_weights,
    approx,
    average,
    start,
):
    shards = q_set.shape[0]
    rows = momentum.shape[1]
    q_avg = jnp.sum(q_set[...], 0) / shards
    p_high, p_mid, p_low = pieces(p_hat[0])
    q_high, q_mid, q_low = pieces(q_avg)
    left = jnp.concatenate([p_high, p_high, p_high, p_mid, p_mid, p_low], 0)
    right = jnp.concatenate([q_high, q_mid, q_low, q_high, q_mid, q_high], 0)
    approx[...] = lax.dot_general(left, right, (((0,), (0,)), ((), ())), preferred_element_type=f32)
    new_error[0] = (grads[0].astype(f32) + errors[0].astype(f32) - approx[...]).astype(jnp.bfloat16)
    new_weights[0] = base[...].reshape(approx.shape) - step_size * approx[...]
    own = pl.ds(pl.multiple_of(index[0] * rows, 8), rows)
    new_momentum[0] = momentum_decay * momentum[0] + approx[own]

    @pl.when(pl.program_id(0) == 0)
    def _():
        columns = router_momentum.shape[0]
        gains = gain_momentum.shape[0]
        blocks = average.shape[1] // lanes
        count = columns + gains
        for i in range(blocks):
            cut = slice(i * lanes, (i + 1) * lanes)
            average[:columns, cut] = small[i * columns : (i + 1) * columns] / shards
            row = blocks * columns + i * gains
            average[columns:count, cut] = small[row : row + gains] / shards
        mine = jnp.zeros((count, rows), f32)
        for i in range(shards):
            cut = slice(i * rows, (i + 1) * rows)
            start[:count, cut] = small_base[i, :count, :rows]
            mine = jnp.where(index[0] == i, average[:count, cut], mine)
        new_router_weights[...] = start[:columns] - step_size * average[:columns]
        new_gain_weights[...] = start[columns:count] - step_size * average[columns:count]
        new_router_momentum[...] = momentum_decay * router_momentum[...] + mine[:columns]
        new_gain_momentum[...] = momentum_decay * gain_momentum[...] + mine[columns:]


def per_device(
    replica_grads,
    error_feedback,
    q_start,
    gram_root,
    momentum,
    weights,
    router_partials,
    gain_partials,
    router_momentum,
    router_weights,
    gain_momentum,
    gain_weights,
):
    shard_count = lax.axis_size(shards)
    section_count = lax.axis_size("sections")
    layer_count = lax.axis_size(layer)
    strip_count = 2 * layer_count
    core = lax.axis_index("core")
    index = lax.axis_index(shards).astype(jnp.int32)[None]
    pairs, rows = momentum.shape[1:3]
    columns = router_weights.shape[1]
    gains = gain_weights.shape[0]
    width = gain_partials.shape[2]
    held = pairs * rows + padded_columns

    base, strips = pl.pallas_call(
        prepare_kernel,
        out_shape=(
            jax.ShapeDtypeStruct((held, lanes), f32),
            jax.ShapeDtypeStruct((strip_count * section_count, lanes), f32),
        ),
        name="prepare",
    )(
        weights.reshape(pairs * rows, lanes),
        momentum.reshape(pairs * rows, lanes),
        router_weights.T,
        router_momentum.T,
        gain_weights,
        gain_momentum,
        router_partials[0].T,
        gain_partials[0],
    )
    base = lax.all_gather(base, shards, axis=0, tiled=False)

    strips = exchange(strips.reshape(section_count, strip_count, lanes), "sections").sum(0)
    combined = replica_grads[0, 0].astype(f32) + error_feedback[0, 0].astype(f32)
    q_rows = q_start[0].transpose(0, 2, 1)
    p_rows = jnp.einsum("krf,kdf->krd", q_rows, combined, precision=highest)
    kept = lax.dynamic_index_in_dim(p_rows, core, 0, keepdims=False)
    sent = lax.dynamic_index_in_dim(p_rows, 1 - core, 0, keepdims=False)
    sent = lax.all_gather(sent, "core", axis=0, tiled=False)
    p_rows = kept + lax.dynamic_index_in_dim(sent, 1 - core, 0, keepdims=False)
    packed = jnp.concatenate([p_rows, strips.reshape(layer_count, 2 * lanes)], 1)
    packed = exchange(packed, layer).sum(0, keepdims=True)
    packed = spread(packed, layer_count, layer)
    packed = lax.all_gather(packed, "core", axis=0, tiled=False)
    strips = packed[:, :, width:].sum(0).reshape(1, strip_count, lanes)
    small = spread(strips, section_count, "sections")

    p_avg = packed[:, :, :width] / shard_count
    p_hat = jnp.einsum("krd,krt->ktd", p_avg, gram_root[0], precision=highest)
    q_local = jnp.einsum("ktd,kdf->ktf", p_hat, combined, precision=highest)
    bundle = q_local.reshape(pairs * rank, lanes)
    bundle, base = lax.optimization_barrier((bundle, base))
    q_set = lax.all_gather(bundle, shards, axis=0, tiled=False)
    q_set, small = lax.optimization_barrier((q_set, small))

    def whole(*shape):
        return pl.BlockSpec(shape, lambda k, _: (0,) * len(shape))

    def kth(*shape):
        return pl.BlockSpec((1,) + shape, lambda k, _: (k,) + (0,) * len(shape))

    new_error, new_momentum, new_weights, router_step, router_new, gain_step, gain_new = pl.pallas_call(
        finish_kernel,
        grid_spec=pltpu.PrefetchScalarGridSpec(
            num_scalar_prefetch=1,
            grid=(pairs,),
            in_specs=[
                pl.BlockSpec((shard_count, rank, lanes), lambda k, _: (0, k, 0)),
                kth(rank, width),
                kth(width, lanes),
                kth(width, lanes),
                pl.BlockSpec((shard_count, rows, lanes), lambda k, _: (0, k, 0)),
                pl.BlockSpec(
                    (shard_count, padded_columns, lanes), lambda k, _: (0, pairs * rows // padded_columns, 0)
                ),
                kth(rows, lanes),
                whole(strip_count * section_count, lanes),
                whole(columns, rows),
                whole(gains, rows),
            ],
            out_specs=[
                kth(width, lanes),
                kth(rows, lanes),
                kth(width, lanes),
                whole(columns, rows),
                whole(columns, width),
                whole(gains, rows),
                whole(gains, width),
            ],
            scratch_shapes=[
                pltpu.VMEM((width, lanes), f32),
                pltpu.VMEM((padded_columns, width), f32),
                pltpu.VMEM((padded_columns, width), f32),
            ],
        ),
        out_shape=(
            jax.ShapeDtypeStruct((pairs, width, lanes), jnp.bfloat16),
            jax.ShapeDtypeStruct((pairs, rows, lanes), f32),
            jax.ShapeDtypeStruct((pairs, width, lanes), f32),
            jax.ShapeDtypeStruct((columns, rows), f32),
            jax.ShapeDtypeStruct((columns, width), f32),
            jax.ShapeDtypeStruct((gains, rows), f32),
            jax.ShapeDtypeStruct((gains, width), f32),
        ),
        name="finish",
    )(
        index,
        q_set,
        p_hat,
        replica_grads[0, 0],
        error_feedback[0, 0],
        base,
        base,
        momentum[0],
        small.reshape(strip_count * section_count, lanes),
        router_momentum.T,
        gain_momentum,
    )
    return (
        new_error[None, None],
        new_momentum[None],
        new_weights[None],
        router_step.T,
        router_new.T,
        gain_step,
        gain_new,
    )


def solution(mesh):
    count, *others = mesh.devices.shape
    split = Mesh(mesh.devices.reshape(count // 2, 2, *others), ("stack", "core", "tensor", "sections"))
    return jax.shard_map(
        per_device,
        mesh=split,
        in_specs=(
            P(shards, "sections", None, None, "tensor"),
            P(shards, "sections", None, None, "tensor"),
            P("sections", None, "tensor", None),
            P("sections", None, None, None),
            P("sections", None, shards, "tensor"),
            P("sections", None, shards, "tensor"),
            P(("stack", "core", "tensor", "sections"), None, None),
            P(("stack", "core", "tensor", "sections"), None, None),
            P(shards, None),
            P(shards, None),
            P(None, shards),
            P(None, shards),
        ),
        out_specs=(
            P(shards, "sections", None, None, "tensor"),
            P("sections", None, shards, "tensor"),
            P("sections", None, None, "tensor"),
            P(shards, None),
            P(),
            P(None, shards),
            P(),
        ),
        check_vma=False,
    )
```

```python
import jax
import jax.numpy as jnp
from jax import lax
from jax.experimental import pallas as pl
from jax.experimental.pallas import tpu as pltpu
from jax.sharding import Mesh
from jax.sharding import PartitionSpec as P

momentum_decay = 0.9
step_size = 0.5
decayed_step = step_size * momentum_decay
lanes = 128
rank = 32
padded_columns = 48
finish_vmem = 51 << 20
highest = lax.Precision.HIGHEST
f32 = jnp.float32
shards = ("stack", "core")
layer = ("stack", "tensor")


def exchange(blocks, axes):
    return lax.all_to_all(blocks, axes, 0, 0, tiled=True)


def spread(row, count, axes):
    return exchange(jnp.broadcast_to(row, (count,) + row.shape[1:]), axes)


def prepare_kernel(
    weights, momentum, router_weights, router_momentum, gain_weights, gain_momentum, router, gain, base, strips
):
    rows = weights.shape[0]
    columns, part = router_weights.shape
    gains = gain_weights.shape[0]
    base[:rows] = weights[...] - decayed_step * momentum[...]
    base[rows:] = jnp.zeros((padded_columns, lanes), f32)
    base[rows : rows + columns, :part] = router_weights[...] - decayed_step * router_momentum[...]
    base[rows + columns : rows + columns + gains, :part] = gain_weights[...] - decayed_step * gain_momentum[...]
    blocks = router.shape[1] // lanes
    strips[blocks * (columns + gains) :] = jnp.zeros((strips.shape[0] - blocks * (columns + gains), lanes), f32)
    for i in range(blocks):
        cut = slice(i * lanes, (i + 1) * lanes)
        strips[i * columns : (i + 1) * columns] = router[:, cut].astype(f32)
        row = blocks * columns + i * gains
        strips[row : row + gains] = gain[:, cut].astype(f32)


def pieces(value):
    high = value.astype(jnp.bfloat16)
    rest = value - high.astype(f32)
    mid = rest.astype(jnp.bfloat16)
    return high, mid, (rest - mid.astype(f32)).astype(jnp.bfloat16)


def finish_kernel(
    index,
    q_set,
    p_hat,
    grads,
    errors,
    base,
    small_base,
    momentum,
    small,
    router_momentum,
    gain_momentum,
    new_error,
    new_momentum,
    new_weights,
    new_router_momentum,
    new_router_weights,
    new_gain_momentum,
    new_gain_weights,
    approx,
    average,
    start,
):
    shards = q_set.shape[0]
    rows = momentum.shape[1]
    q_avg = jnp.sum(q_set[...], 0) / shards
    p_high, p_mid, p_low = pieces(p_hat[0])
    q_high, q_mid, q_low = pieces(q_avg)
    left = jnp.concatenate([p_high, p_high, p_high, p_mid, p_mid, p_low], 0)
    right = jnp.concatenate([q_high, q_mid, q_low, q_high, q_mid, q_high], 0)
    approx[...] = lax.dot_general(left, right, (((0,), (0,)), ((), ())), preferred_element_type=f32)
    new_error[0] = (grads[0].astype(f32) + errors[0].astype(f32) - approx[...]).astype(jnp.bfloat16)
    new_weights[0] = base[...].reshape(approx.shape) - step_size * approx[...]
    own = pl.ds(pl.multiple_of(index[0] * rows, 8), rows)
    new_momentum[0] = momentum_decay * momentum[0] + approx[own]

    @pl.when(pl.program_id(0) == 0)
    def _():
        columns = router_momentum.shape[0]
        gains = gain_momentum.shape[0]
        blocks = average.shape[1] // lanes
        count = columns + gains
        for i in range(blocks):
            cut = slice(i * lanes, (i + 1) * lanes)
            average[:columns, cut] = small[i * columns : (i + 1) * columns] / shards
            row = blocks * columns + i * gains
            average[columns:count, cut] = small[row : row + gains] / shards
        mine = jnp.zeros((count, rows), f32)
        for i in range(shards):
            cut = slice(i * rows, (i + 1) * rows)
            start[:count, cut] = small_base[i, :count, :rows]
            mine = jnp.where(index[0] == i, average[:count, cut], mine)
        new_router_weights[...] = start[:columns] - step_size * average[:columns]
        new_gain_weights[...] = start[columns:count] - step_size * average[columns:count]
        new_router_momentum[...] = momentum_decay * router_momentum[...] + mine[:columns]
        new_gain_momentum[...] = momentum_decay * gain_momentum[...] + mine[columns:]


def per_device(
    replica_grads,
    error_feedback,
    q_start,
    gram_root,
    momentum,
    weights,
    router_partials,
    gain_partials,
    router_momentum,
    router_weights,
    gain_momentum,
    gain_weights,
):
    shard_count = lax.axis_size(shards)
    section_count = lax.axis_size("sections")
    layer_count = lax.axis_size(layer)
    strip_count = 2 * layer_count
    core = lax.axis_index("core")
    index = lax.axis_index(shards).astype(jnp.int32)[None]
    pairs, rows = momentum.shape[1:3]
    columns = router_weights.shape[1]
    gains = gain_weights.shape[0]
    width = gain_partials.shape[2]
    held = pairs * rows + padded_columns

    base, strips = pl.pallas_call(
        prepare_kernel,
        out_shape=(
            jax.ShapeDtypeStruct((held, lanes), f32),
            jax.ShapeDtypeStruct((strip_count * section_count, lanes), f32),
        ),
        name="prepare",
    )(
        weights.reshape(pairs * rows, lanes),
        momentum.reshape(pairs * rows, lanes),
        router_weights.T,
        router_momentum.T,
        gain_weights,
        gain_momentum,
        router_partials[0].T,
        gain_partials[0],
    )
    base = lax.all_gather(base, shards, axis=0, tiled=False)

    strips = exchange(strips.reshape(section_count, strip_count, lanes), "sections").sum(0)
    combined = replica_grads[0, 0].astype(f32) + error_feedback[0, 0].astype(f32)
    q_rows = q_start[0].transpose(0, 2, 1)
    p_rows = jnp.einsum("krf,kdf->krd", q_rows, combined, precision=highest)
    kept = lax.dynamic_index_in_dim(p_rows, core, 0, keepdims=False)
    sent = lax.dynamic_index_in_dim(p_rows, 1 - core, 0, keepdims=False)
    sent = lax.all_gather(sent, "core", axis=0, tiled=False)
    p_rows = kept + lax.dynamic_index_in_dim(sent, 1 - core, 0, keepdims=False)
    packed = jnp.concatenate([p_rows, strips.reshape(layer_count, 2 * lanes)], 1)
    packed = exchange(packed, layer).sum(0, keepdims=True)
    packed = spread(packed, layer_count, layer)
    packed = lax.all_gather(packed, "core", axis=0, tiled=False)
    strips = packed[:, :, width:].sum(0).reshape(1, strip_count, lanes)
    small = spread(strips, section_count, "sections")

    p_avg = packed[:, :, :width] / shard_count
    p_hat = jnp.einsum("krd,krt->ktd", p_avg, gram_root[0], precision=highest)
    q_local = jnp.einsum("ktd,kdf->ktf", p_hat, combined, precision=highest)
    bundle = q_local.reshape(pairs * rank, lanes)
    bundle, base = lax.optimization_barrier((bundle, base))
    q_set = lax.all_gather(bundle, shards, axis=0, tiled=False)
    q_set, small = lax.optimization_barrier((q_set, small))

    def whole(*shape):
        return pl.BlockSpec(shape, lambda k, _: (0,) * len(shape))

    def kth(*shape):
        return pl.BlockSpec((1,) + shape, lambda k, _: (k,) + (0,) * len(shape))

    new_error, new_momentum, new_weights, router_step, router_new, gain_step, gain_new = pl.pallas_call(
        finish_kernel,
        grid_spec=pltpu.PrefetchScalarGridSpec(
            num_scalar_prefetch=1,
            grid=(pairs,),
            in_specs=[
                pl.BlockSpec((shard_count, rank, lanes), lambda k, _: (0, k, 0)),
                kth(rank, width),
                kth(width, lanes),
                kth(width, lanes),
                pl.BlockSpec((shard_count, rows, lanes), lambda k, _: (0, k, 0)),
                pl.BlockSpec(
                    (shard_count, padded_columns, lanes), lambda k, _: (0, pairs * rows // padded_columns, 0)
                ),
                kth(rows, lanes),
                whole(strip_count * section_count, lanes),
                whole(columns, rows),
                whole(gains, rows),
            ],
            out_specs=[
                kth(width, lanes),
                kth(rows, lanes),
                kth(width, lanes),
                whole(columns, rows),
                whole(columns, width),
                whole(gains, rows),
                whole(gains, width),
            ],
            scratch_shapes=[
                pltpu.VMEM((width, lanes), f32),
                pltpu.VMEM((padded_columns, width), f32),
                pltpu.VMEM((padded_columns, width), f32),
            ],
        ),
        out_shape=(
            jax.ShapeDtypeStruct((pairs, width, lanes), jnp.bfloat16),
            jax.ShapeDtypeStruct((pairs, rows, lanes), f32),
            jax.ShapeDtypeStruct((pairs, width, lanes), f32),
            jax.ShapeDtypeStruct((columns, rows), f32),
            jax.ShapeDtypeStruct((columns, width), f32),
            jax.ShapeDtypeStruct((gains, rows), f32),
            jax.ShapeDtypeStruct((gains, width), f32),
        ),
        compiler_params=pltpu.CompilerParams(vmem_limit_bytes=finish_vmem),
        name="finish",
    )(
        index,
        q_set,
        p_hat,
        replica_grads[0, 0],
        error_feedback[0, 0],
        base,
        base,
        momentum[0],
        small.reshape(strip_count * section_count, lanes),
        router_momentum.T,
        gain_momentum,
    )
    return (
        new_error[None, None],
        new_momentum[None],
        new_weights[None],
        router_step.T,
        router_new.T,
        gain_step,
        gain_new,
    )


def solution(mesh):
    count, *others = mesh.devices.shape
    split = Mesh(mesh.devices.reshape(count // 2, 2, *others), ("stack", "core", "tensor", "sections"))
    return jax.shard_map(
        per_device,
        mesh=split,
        in_specs=(
            P(shards, "sections", None, None, "tensor"),
            P(shards, "sections", None, None, "tensor"),
            P("sections", None, "tensor", None),
            P("sections", None, None, None),
            P("sections", None, shards, "tensor"),
            P("sections", None, shards, "tensor"),
            P(("stack", "core", "tensor", "sections"), None, None),
            P(("stack", "core", "tensor", "sections"), None, None),
            P(shards, None),
            P(shards, None),
            P(None, shards),
            P(None, shards),
        ),
        out_specs=(
            P(shards, "sections", None, None, "tensor"),
            P("sections", None, shards, "tensor"),
            P("sections", None, None, "tensor"),
            P(shards, None),
            P(),
            P(None, shards),
            P(),
        ),
        check_vma=False,
    )
```

```python
import jax
import jax.numpy as jnp
from jax import lax
from jax.experimental import pallas as pl
from jax.experimental.pallas import tpu as pltpu
from jax.sharding import Mesh
from jax.sharding import PartitionSpec as P

momentum_decay = 0.9
step_size = 0.5
decayed_step = step_size * momentum_decay
lanes = 128
rank = 32
padded_columns = 48
finish_vmem = 51 << 20
highest = lax.Precision.HIGHEST
f32 = jnp.float32
shards = ("stack", "core")
layer = ("stack", "tensor")


def exchange(blocks, axes):
    return lax.all_to_all(blocks, axes, 0, 0, tiled=True)


def spread(row, count, axes):
    return exchange(jnp.broadcast_to(row, (count,) + row.shape[1:]), axes)


def prepare_kernel(
    weights, momentum, router_weights, router_momentum, gain_weights, gain_momentum, router, gain, base, strips
):
    rows = weights.shape[0]
    columns, part = router_weights.shape
    gains = gain_weights.shape[0]
    base[:rows] = weights[...] - decayed_step * momentum[...]
    base[rows:] = jnp.zeros((padded_columns, lanes), f32)
    base[rows : rows + columns, :part] = router_weights[...] - decayed_step * router_momentum[...]
    base[rows + columns : rows + columns + gains, :part] = gain_weights[...] - decayed_step * gain_momentum[...]
    blocks = router.shape[1] // lanes
    strips[blocks * (columns + gains) :] = jnp.zeros((strips.shape[0] - blocks * (columns + gains), lanes), f32)
    for i in range(blocks):
        cut = slice(i * lanes, (i + 1) * lanes)
        strips[i * columns : (i + 1) * columns] = router[:, cut].astype(f32)
        row = blocks * columns + i * gains
        strips[row : row + gains] = gain[:, cut].astype(f32)


def pieces(value):
    high = value.astype(jnp.bfloat16)
    rest = value - high.astype(f32)
    mid = rest.astype(jnp.bfloat16)
    return high, mid, (rest - mid.astype(f32)).astype(jnp.bfloat16)


def finish_kernel(
    index,
    q_set,
    p_hat,
    grads,
    errors,
    base,
    small_base,
    momentum,
    small,
    router_momentum,
    gain_momentum,
    new_error,
    new_momentum,
    new_weights,
    new_router_momentum,
    new_router_weights,
    new_gain_momentum,
    new_gain_weights,
    approx,
    average,
    start,
):
    shards = q_set.shape[0]
    rows = momentum.shape[1]
    q_avg = jnp.sum(q_set[...], 0) / shards
    p_high, p_mid, p_low = pieces(p_hat[0])
    q_high, q_mid, q_low = pieces(q_avg)
    left = jnp.concatenate([p_high, p_high, p_high, p_mid, p_mid, p_low], 0)
    right = jnp.concatenate([q_high, q_mid, q_low, q_high, q_mid, q_high], 0)
    approx[...] = lax.dot_general(left, right, (((0,), (0,)), ((), ())), preferred_element_type=f32)
    new_error[0] = (grads[0].astype(f32) + errors[0].astype(f32) - approx[...]).astype(jnp.bfloat16)
    new_weights[0] = base[...].reshape(approx.shape) - step_size * approx[...]
    own = pl.ds(pl.multiple_of(index[0] * rows, 8), rows)
    new_momentum[0] = momentum_decay * momentum[0] + approx[own]

    @pl.when(pl.program_id(0) == 0)
    def _():
        columns = router_momentum.shape[0]
        gains = gain_momentum.shape[0]
        blocks = average.shape[1] // lanes
        count = columns + gains
        for i in range(blocks):
            cut = slice(i * lanes, (i + 1) * lanes)
            average[:columns, cut] = small[i * columns : (i + 1) * columns] / shards
            row = blocks * columns + i * gains
            average[columns:count, cut] = small[row : row + gains] / shards
        for i in range(shards):
            cut = slice(i * rows, (i + 1) * rows)
            start[:count, cut] = small_base[i, :count, :rows]

            @pl.when(index[0] == i)
            def _():
                new_router_momentum[...] = momentum_decay * router_momentum[...] + average[:columns, cut]
                new_gain_momentum[...] = momentum_decay * gain_momentum[...] + average[columns:count, cut]

        new_router_weights[...] = start[:columns] - step_size * average[:columns]
        new_gain_weights[...] = start[columns:count] - step_size * average[columns:count]


def per_device(
    replica_grads,
    error_feedback,
    q_start,
    gram_root,
    momentum,
    weights,
    router_partials,
    gain_partials,
    router_momentum,
    router_weights,
    gain_momentum,
    gain_weights,
):
    shard_count = lax.axis_size(shards)
    section_count = lax.axis_size("sections")
    layer_count = lax.axis_size(layer)
    strip_count = 2 * layer_count
    core = lax.axis_index("core")
    index = lax.axis_index(shards).astype(jnp.int32)[None]
    pairs, rows = momentum.shape[1:3]
    columns = router_weights.shape[1]
    gains = gain_weights.shape[0]
    width = gain_partials.shape[2]
    held = pairs * rows + padded_columns

    base, strips = pl.pallas_call(
        prepare_kernel,
        out_shape=(
            jax.ShapeDtypeStruct((held, lanes), f32),
            jax.ShapeDtypeStruct((strip_count * section_count, lanes), f32),
        ),
        name="prepare",
    )(
        weights.reshape(pairs * rows, lanes),
        momentum.reshape(pairs * rows, lanes),
        router_weights.T,
        router_momentum.T,
        gain_weights,
        gain_momentum,
        router_partials[0].T,
        gain_partials[0],
    )
    base = lax.all_gather(base, shards, axis=0, tiled=False)

    strips = exchange(strips.reshape(section_count, strip_count, lanes), "sections").sum(0)
    combined = replica_grads[0, 0].astype(f32) + error_feedback[0, 0].astype(f32)
    q_rows = q_start[0].transpose(0, 2, 1)
    q_high = lax.reduce_precision(q_rows, 8, 7)
    q_mid = lax.reduce_precision(q_rows - q_high, 8, 7)
    q_set = jnp.concatenate([q_high, q_mid, q_rows - q_high - q_mid], 1).astype(jnp.bfloat16)
    p_set = jnp.einsum("krf,kdf->krd", q_set, replica_grads[0, 0], preferred_element_type=f32)
    p_set += jnp.einsum("krf,kdf->krd", q_set, error_feedback[0, 0], preferred_element_type=f32)
    p_rows = p_set.reshape(pairs, 3, rank, width).sum(1)
    kept = lax.dynamic_index_in_dim(p_rows, core, 0, keepdims=False)
    sent = lax.dynamic_index_in_dim(p_rows, 1 - core, 0, keepdims=False)
    sent = lax.all_gather(sent, "core", axis=0, tiled=False)
    p_rows = kept + lax.dynamic_index_in_dim(sent, 1 - core, 0, keepdims=False)
    packed = jnp.concatenate([p_rows, strips.reshape(layer_count, 2 * lanes)], 1)
    packed = exchange(packed, layer).sum(0, keepdims=True)
    packed = spread(packed, layer_count, layer)
    packed = lax.all_gather(packed, "core", axis=0, tiled=False)
    strips = packed[:, :, width:].sum(0).reshape(1, strip_count, lanes)
    small = spread(strips, section_count, "sections")

    p_avg = packed[:, :, :width] / shard_count
    p_hat = jnp.einsum("krd,krt->ktd", p_avg, gram_root[0], precision=highest)
    q_local = jnp.einsum("ktd,kdf->ktf", p_hat, combined, precision=highest)
    bundle = q_local.reshape(pairs * rank, lanes)
    bundle, base = lax.optimization_barrier((bundle, base))
    q_set = lax.all_gather(bundle, shards, axis=0, tiled=False)
    q_set, small = lax.optimization_barrier((q_set, small))

    def whole(*shape):
        return pl.BlockSpec(shape, lambda k, _: (0,) * len(shape))

    def kth(*shape):
        return pl.BlockSpec((1,) + shape, lambda k, _: (k,) + (0,) * len(shape))

    new_error, new_momentum, new_weights, router_step, router_new, gain_step, gain_new = pl.pallas_call(
        finish_kernel,
        grid_spec=pltpu.PrefetchScalarGridSpec(
            num_scalar_prefetch=1,
            grid=(pairs,),
            in_specs=[
                pl.BlockSpec((shard_count, rank, lanes), lambda k, _: (0, k, 0)),
                kth(rank, width),
                kth(width, lanes),
                kth(width, lanes),
                pl.BlockSpec((shard_count, rows, lanes), lambda k, _: (0, k, 0)),
                pl.BlockSpec(
                    (shard_count, padded_columns, lanes), lambda k, _: (0, pairs * rows // padded_columns, 0)
                ),
                kth(rows, lanes),
                whole(strip_count * section_count, lanes),
                whole(columns, rows),
                whole(gains, rows),
            ],
            out_specs=[
                kth(width, lanes),
                kth(rows, lanes),
                kth(width, lanes),
                whole(columns, rows),
                whole(columns, width),
                whole(gains, rows),
                whole(gains, width),
            ],
            scratch_shapes=[
                pltpu.VMEM((width, lanes), f32),
                pltpu.VMEM((padded_columns, width), f32),
                pltpu.VMEM((padded_columns, width), f32),
            ],
        ),
        out_shape=(
            jax.ShapeDtypeStruct((pairs, width, lanes), jnp.bfloat16),
            jax.ShapeDtypeStruct((pairs, rows, lanes), f32),
            jax.ShapeDtypeStruct((pairs, width, lanes), f32),
            jax.ShapeDtypeStruct((columns, rows), f32),
            jax.ShapeDtypeStruct((columns, width), f32),
            jax.ShapeDtypeStruct((gains, rows), f32),
            jax.ShapeDtypeStruct((gains, width), f32),
        ),
        compiler_params=pltpu.CompilerParams(vmem_limit_bytes=finish_vmem),
        name="finish",
    )(
        index,
        q_set,
        p_hat,
        replica_grads[0, 0],
        error_feedback[0, 0],
        base,
        base,
        momentum[0],
        small.reshape(strip_count * section_count, lanes),
        router_momentum.T,
        gain_momentum,
    )
    return (
        new_error[None, None],
        new_momentum[None],
        new_weights[None],
        router_step.T,
        router_new.T,
        gain_step,
        gain_new,
    )


def solution(mesh):
    count, *others = mesh.devices.shape
    split = Mesh(mesh.devices.reshape(count // 2, 2, *others), ("stack", "core", "tensor", "sections"))
    return jax.shard_map(
        per_device,
        mesh=split,
        in_specs=(
            P(shards, "sections", None, None, "tensor"),
            P(shards, "sections", None, None, "tensor"),
            P("sections", None, "tensor", None),
            P("sections", None, None, None),
            P("sections", None, shards, "tensor"),
            P("sections", None, shards, "tensor"),
            P(("stack", "core", "tensor", "sections"), None, None),
            P(("stack", "core", "tensor", "sections"), None, None),
            P(shards, None),
            P(shards, None),
            P(None, shards),
            P(None, shards),
        ),
        out_specs=(
            P(shards, "sections", None, None, "tensor"),
            P("sections", None, shards, "tensor"),
            P("sections", None, None, "tensor"),
            P(shards, None),
            P(),
            P(None, shards),
            P(),
        ),
        check_vma=False,
    )
```

```python
import jax
import jax.numpy as jnp
from jax import lax
from jax.experimental import pallas as pl
from jax.experimental.pallas import tpu as pltpu
from jax.sharding import Mesh
from jax.sharding import PartitionSpec as P

momentum_decay = 0.9
step_size = 0.5
decayed_step = step_size * momentum_decay
lanes = 128
rank = 32
padded_columns = 48
finish_vmem = 24 << 20
highest = lax.Precision.HIGHEST
f32 = jnp.float32
shards = ("stack", "core")
layer = ("stack", "tensor")


def exchange(blocks, axes):
    return lax.all_to_all(blocks, axes, 0, 0, tiled=True)


def spread(row, count, axes):
    return exchange(jnp.broadcast_to(row, (count,) + row.shape[1:]), axes)


def prepare_kernel(
    weights, momentum, router_weights, router_momentum, gain_weights, gain_momentum, router, gain, base, strips
):
    rows = weights.shape[0]
    columns, part = router_weights.shape
    gains = gain_weights.shape[0]
    base[:rows] = weights[...] - decayed_step * momentum[...]
    base[rows:] = jnp.zeros((padded_columns, lanes), f32)
    base[rows : rows + columns, :part] = router_weights[...] - decayed_step * router_momentum[...]
    base[rows + columns : rows + columns + gains, :part] = gain_weights[...] - decayed_step * gain_momentum[...]
    blocks = router.shape[1] // lanes
    strips[blocks * (columns + gains) :] = jnp.zeros((strips.shape[0] - blocks * (columns + gains), lanes), f32)
    for i in range(blocks):
        cut = slice(i * lanes, (i + 1) * lanes)
        strips[i * columns : (i + 1) * columns] = router[:, cut].astype(f32)
        row = blocks * columns + i * gains
        strips[row : row + gains] = gain[:, cut].astype(f32)


def pieces(value):
    high = value.astype(jnp.bfloat16)
    rest = value - high.astype(f32)
    mid = rest.astype(jnp.bfloat16)
    return high, mid, (rest - mid.astype(f32)).astype(jnp.bfloat16)


def finish_kernel(
    index,
    q_set,
    p_hat,
    grads,
    errors,
    base,
    small_base,
    momentum,
    small,
    router_momentum,
    gain_momentum,
    new_error,
    new_momentum,
    new_weights,
    new_router_momentum,
    new_router_weights,
    new_gain_momentum,
    new_gain_weights,
    approx,
    average,
    start,
):
    shards = q_set.shape[0]
    rows = momentum.shape[1]
    q_avg = jnp.sum(q_set[...], 0) / shards
    p_high, p_mid, p_low = pieces(p_hat[0])
    q_high, q_mid, q_low = pieces(q_avg)
    left = jnp.concatenate([p_high, p_high, p_high, p_mid, p_mid, p_low], 0)
    right = jnp.concatenate([q_high, q_mid, q_low, q_high, q_mid, q_high], 0)
    approx[...] = lax.dot_general(left, right, (((0,), (0,)), ((), ())), preferred_element_type=f32)
    new_error[0] = (grads[0].astype(f32) + errors[0].astype(f32) - approx[...]).astype(jnp.bfloat16)
    new_weights[0] = 0.5 * base[...].reshape(approx.shape) - step_size * approx[...]
    own = pl.ds(pl.multiple_of(index[0] * rows, 8), rows)
    new_momentum[0] = momentum_decay * momentum[0] + approx[own]

    @pl.when(pl.program_id(0) == 0)
    def _():
        columns = router_momentum.shape[0]
        gains = gain_momentum.shape[0]
        blocks = average.shape[1] // lanes
        count = columns + gains
        for i in range(blocks):
            cut = slice(i * lanes, (i + 1) * lanes)
            average[:columns, cut] = small[i * columns : (i + 1) * columns] / shards
            row = blocks * columns + i * gains
            average[columns:count, cut] = small[row : row + gains] / shards
        for i in range(shards):
            cut = slice(i * rows, (i + 1) * rows)
            start[:count, cut] = 0.5 * small_base[i, :count, :rows]

            @pl.when(index[0] == i)
            def _():
                new_router_momentum[...] = momentum_decay * router_momentum[...] + average[:columns, cut]
                new_gain_momentum[...] = momentum_decay * gain_momentum[...] + average[columns:count, cut]

        new_router_weights[...] = start[:columns] - step_size * average[:columns]
        new_gain_weights[...] = start[columns:count] - step_size * average[columns:count]


def per_device(
    replica_grads,
    error_feedback,
    q_start,
    gram_root,
    momentum,
    weights,
    router_partials,
    gain_partials,
    router_momentum,
    router_weights,
    gain_momentum,
    gain_weights,
):
    shard_count = lax.axis_size(shards)
    section_count = lax.axis_size("sections")
    layer_count = lax.axis_size(layer)
    strip_count = 2 * layer_count
    core = lax.axis_index("core")
    index = lax.axis_index(shards).astype(jnp.int32)[None]
    pairs, rows = momentum.shape[1:3]
    columns = router_weights.shape[1]
    gains = gain_weights.shape[0]
    width = gain_partials.shape[2]
    held = pairs * rows + padded_columns

    base, strips = pl.pallas_call(
        prepare_kernel,
        out_shape=(
            jax.ShapeDtypeStruct((held, lanes), f32),
            jax.ShapeDtypeStruct((strip_count * section_count, lanes), f32),
        ),
        name="prepare",
    )(
        weights.reshape(pairs * rows, lanes),
        momentum.reshape(pairs * rows, lanes),
        router_weights.T,
        router_momentum.T,
        gain_weights,
        gain_momentum,
        router_partials[0].T,
        gain_partials[0],
    )
    base = lax.all_gather(base, shards, axis=0, tiled=False)

    strips = exchange(strips.reshape(section_count, strip_count, lanes), "sections").sum(0)
    combined = replica_grads[0, 0].astype(f32) + error_feedback[0, 0].astype(f32)
    q_rows = q_start[0].transpose(0, 2, 1)
    q_high = lax.reduce_precision(q_rows, 8, 7)
    q_mid = lax.reduce_precision(q_rows - q_high, 8, 7)
    q_set = jnp.concatenate([q_high, q_mid, q_rows - q_high - q_mid], 1).astype(jnp.bfloat16)
    p_set = jnp.einsum("krf,kdf->krd", q_set, replica_grads[0, 0], preferred_element_type=f32)
    p_set += jnp.einsum("krf,kdf->krd", q_set, error_feedback[0, 0], preferred_element_type=f32)
    p_rows = p_set.reshape(pairs, 3, rank, width).sum(1)
    kept = lax.dynamic_index_in_dim(p_rows, core, 0, keepdims=False)
    sent = lax.dynamic_index_in_dim(p_rows, 1 - core, 0, keepdims=False)
    sent = lax.all_gather(sent, "core", axis=0, tiled=False)
    p_rows = kept + lax.dynamic_index_in_dim(sent, 1 - core, 0, keepdims=False)
    packed = jnp.concatenate([p_rows, strips.reshape(layer_count, 2 * lanes)], 1)
    packed = exchange(packed, layer).sum(0, keepdims=True)
    packed = spread(packed, layer_count, layer)
    packed, base = lax.optimization_barrier((packed, 2.0 * base))
    packed = lax.all_gather(packed, "core", axis=0, tiled=False)
    strips = packed[:, :, width:].sum(0).reshape(1, strip_count, lanes)
    small = spread(strips, section_count, "sections")

    p_avg = packed[:, :, :width] / shard_count
    p_hat = jnp.einsum("krd,krt->ktd", p_avg, gram_root[0], precision=highest)
    q_local = jnp.einsum("ktd,kdf->ktf", p_hat, combined, precision=highest)
    bundle = q_local.reshape(pairs * rank, lanes)
    q_set = lax.all_gather(bundle, shards, axis=0, tiled=False)
    q_set, small = lax.optimization_barrier((q_set, small))

    def whole(*shape):
        return pl.BlockSpec(shape, lambda k, _: (0,) * len(shape))

    def kth(*shape):
        return pl.BlockSpec((1,) + shape, lambda k, _: (k,) + (0,) * len(shape))

    new_error, new_momentum, new_weights, router_step, router_new, gain_step, gain_new = pl.pallas_call(
        finish_kernel,
        grid_spec=pltpu.PrefetchScalarGridSpec(
            num_scalar_prefetch=1,
            grid=(pairs,),
            in_specs=[
                pl.BlockSpec((shard_count, rank, lanes), lambda k, _: (0, k, 0)),
                kth(rank, width),
                kth(width, lanes),
                kth(width, lanes),
                pl.BlockSpec((shard_count, rows, lanes), lambda k, _: (0, k, 0)),
                pl.BlockSpec(
                    (shard_count, padded_columns, lanes), lambda k, _: (0, pairs * rows // padded_columns, 0)
                ),
                kth(rows, lanes),
                whole(strip_count * section_count, lanes),
                whole(columns, rows),
                whole(gains, rows),
            ],
            out_specs=[
                kth(width, lanes),
                kth(rows, lanes),
                kth(width, lanes),
                whole(columns, rows),
                whole(columns, width),
                whole(gains, rows),
                whole(gains, width),
            ],
            scratch_shapes=[
                pltpu.VMEM((width, lanes), f32),
                pltpu.VMEM((padded_columns, width), f32),
                pltpu.VMEM((padded_columns, width), f32),
            ],
        ),
        out_shape=(
            jax.ShapeDtypeStruct((pairs, width, lanes), jnp.bfloat16),
            jax.ShapeDtypeStruct((pairs, rows, lanes), f32),
            jax.ShapeDtypeStruct((pairs, width, lanes), f32),
            jax.ShapeDtypeStruct((columns, rows), f32),
            jax.ShapeDtypeStruct((columns, width), f32),
            jax.ShapeDtypeStruct((gains, rows), f32),
            jax.ShapeDtypeStruct((gains, width), f32),
        ),
        compiler_params=pltpu.CompilerParams(vmem_limit_bytes=finish_vmem),
        name="finish",
    )(
        index,
        q_set,
        p_hat,
        replica_grads[0, 0],
        error_feedback[0, 0],
        base,
        base,
        momentum[0],
        small.reshape(strip_count * section_count, lanes),
        router_momentum.T,
        gain_momentum,
    )
    return (
        new_error[None, None],
        new_momentum[None],
        new_weights[None],
        router_step.T,
        router_new.T,
        gain_step,
        gain_new,
    )


def solution(mesh):
    count, *others = mesh.devices.shape
    split = Mesh(mesh.devices.reshape(count // 2, 2, *others), ("stack", "core", "tensor", "sections"))
    return jax.shard_map(
        per_device,
        mesh=split,
        in_specs=(
            P(shards, "sections", None, None, "tensor"),
            P(shards, "sections", None, None, "tensor"),
            P("sections", None, "tensor", None),
            P("sections", None, None, None),
            P("sections", None, shards, "tensor"),
            P("sections", None, shards, "tensor"),
            P(("stack", "core", "tensor", "sections"), None, None),
            P(("stack", "core", "tensor", "sections"), None, None),
            P(shards, None),
            P(shards, None),
            P(None, shards),
            P(None, shards),
        ),
        out_specs=(
            P(shards, "sections", None, None, "tensor"),
            P("sections", None, shards, "tensor"),
            P("sections", None, None, "tensor"),
            P(shards, None),
            P(),
            P(None, shards),
            P(),
        ),
        check_vma=False,
    )
```
